1024 devices in a mesh: row: 16 (over z), col: 64 (over y, x, core).
Axes of the slice: x: 4, y: 8, z: 16, core: 2. Of those that a mesh axis runs over, the one named last changes fastest.
Arguments:
- slot_factors: bfloat16 [16, 64, 2, 1024, 256], P('row', 'col'), may hold values from -0.75 to 0.75
- slot_pairs: int32 [16, 64, 2], P('row', 'col'), may hold values from 0 to 2, as said below
- pivot_factors: bfloat16 [32, 1024, 256], P('row', 'col'), may hold values from -0.75 to 0.75
- a_factors: bfloat16 [64, 1024, 256], P('col'), as said below
- diag_factor: float32 [1024, 1024], replicated, as said below
- sketch: float32 [1024, 128], replicated, as said below
Outputs:
- panel_basis: float32 [64, 1024, 128], P('col')
- panel_coeff: float32 [64, 1024, 128], P('col')
The draws below stay inside these ranges and needn't reach their ends.
Inputs may be any that keep to these rules, and one draw needn't show every extreme that they name: `slot_pairs`: on each cell (r, c) the live codes come first, are distinct and below 2; the remaining entries equal 2. Every cell has at least one live slot, and in every draw some cell is full and some cell has exactly one. `diag_factor`: lower triangular; the diagonal lies between 1 and 2. `a_factors`: real values of order one. `sketch`: real values.
All inputs are finite; a program needn't handle non-finite values.
Results may differ from the reference program's by a relative error of at most 0.0003.
Values may be sent and summed in bfloat16 or wider, within the bound.
No kernel may reach another device: no remote copies, remote signals or barrier semaphores. Data moves between devices by JAX's collectives and lax.ppermute only.
A program may use at most 64 MiB of HBM per device.

```python
import jax
import jax.numpy as jnp
from jax import lax

TILE = 1024
RANK = 128
TI = 1
TJ = 2
SLOTS = 2
ROWS_T = 64
COLS_T = 32
N_ROW = 16
N_COL = 64


def draw_slot_pairs(key, part):
    cell_total = N_ROW * N_COL
    key_count, key_perm = jax.random.split(jax.random.fold_in(key, 11))
    counts = jax.random.randint(key_count, (cell_total,), 1, SLOTS + 1)
    counts = counts.at[0].set(SLOTS).at[1].set(1)
    keys = jax.random.split(key_perm, cell_total)
    orderings = jax.vmap(lambda single: jax.random.permutation(single, TI * TJ))(keys)[:, :SLOTS]
    position = jnp.arange(SLOTS)
    pair_codes = jnp.where(position[None, :] < counts[:, None], orderings, TI * TJ)
    return pair_codes.reshape(N_ROW, N_COL, SLOTS).astype(jnp.int32)


def draw_diag_factor(key, part):
    key_below, key_diag = jax.random.split(jax.random.fold_in(key, 23))
    below_part = jax.random.normal(key_below, (TILE, TILE), jnp.float32) * (0.2 / jnp.sqrt(jnp.float32(TILE)))
    diagonal = jnp.exp(jax.random.uniform(key_diag, (TILE,), jnp.float32, 0.0, 0.693))
    factor = jnp.tril(below_part, -1) + jnp.diag(diagonal)
    return factor.astype(jnp.float32)


def joint_panel(key):
    key_sketch, key_left, key_noise = jax.random.split(jax.random.fold_in(key, 37), 3)
    root_tile = jnp.sqrt(jnp.float32(TILE))
    sketch_part = jax.random.normal(key_sketch, (TILE, RANK), jnp.float32) / root_tile
    left_part = jax.random.normal(key_left, (ROWS_T, TILE, RANK), jnp.float32) * 0.5
    noise_part = jax.random.normal(key_noise, (ROWS_T, TILE, RANK), jnp.float32) * 0.1
    right_part = 16.0 * sketch_part[None, :, :] + noise_part
    return (sketch_part, jnp.concatenate([left_part, right_part], axis=-1))


def draw_sketch(key, part):
    sketch_part, panel_part = joint_panel(key)
    return sketch_part.astype(jnp.float32)


def draw_a_factors(key, part):
    sketch_part, panel_part = joint_panel(key)
    return panel_part.astype(jnp.bfloat16)


def block_levels(key, extent, shards, smallest, largest):
    def one(dim, parts):
        draws = jax.random.uniform(jax.random.fold_in(jax.random.fold_in(key, 6), dim), (parts,), jnp.float32, smallest / len(shards), largest / len(shards))
        return jnp.repeat(jnp.exp(draws), extent[dim] // parts).reshape((-1,) + (1,) * (len(extent) - dim - 1))

    gain = one(*shards[0])
    for cut in shards[1:]:
        gain = gain * one(*cut)
    return gain


def scatter_about(key, dims, scale, bound, cuts=(), kind=jnp.bfloat16):
    level = block_levels(key, dims, cuts, -0.22, 0.18) if cuts else 1.0
    result = jax.random.normal(key, dims, jnp.float32) * scale * level
    return jnp.minimum(jnp.maximum(result, -bound), bound).astype(kind)


def setup_inputs(seed: int = 0) -> dict:
    arg_keys = jax.random.split(jax.random.key(seed), 7)
    slot_factors = scatter_about(arg_keys[0], (N_ROW, N_COL, SLOTS, TILE, 2 * RANK), 0.125, 0.75, ((0, 16), (1, 64)))
    slot_pairs = draw_slot_pairs(jax.random.fold_in(arg_keys[6], 71), 0)
    pivot_factors = scatter_about(arg_keys[2], (COLS_T, TILE, 2 * RANK), 0.125, 0.75, ((0, 16), (1, 64)))
    a_factors = draw_a_factors(jax.random.fold_in(arg_keys[6], 71), 0)
    diag_factor = draw_diag_factor(jax.random.fold_in(arg_keys[6], 71), 0)
    sketch = draw_sketch(jax.random.fold_in(arg_keys[6], 71), 0)
    return dict(slot_factors=slot_factors, slot_pairs=slot_pairs, pivot_factors=pivot_factors, a_factors=a_factors, diag_factor=diag_factor, sketch=sketch)


def orthonormal(sketch_rows):
    precise_mode = lax.Precision.HIGHEST
    gram_matrix = jnp.einsum('ibr,ibc->irc', sketch_rows, sketch_rows, precision=precise_mode)
    factor_low = jnp.linalg.cholesky(gram_matrix)
    solved = lax.linalg.triangular_solve(factor_low, jnp.swapaxes(sketch_rows, 1, 2), left_side=True, lower=True)
    return jnp.swapaxes(solved, 1, 2)

def slot_block(slot_factors, slot_pairs, row_index):
    block_data = lax.dynamic_index_in_dim(slot_factors, row_index, 0, keepdims=False).astype(jnp.float32)
    block_data = block_data.reshape(N_COL * SLOTS, TILE, 2 * RANK)
    pair_codes = lax.dynamic_index_in_dim(slot_pairs, row_index, 0, keepdims=False).reshape(-1)
    owner_col = jnp.repeat(jnp.arange(N_COL, dtype=jnp.int32), SLOTS)
    active_flag = pair_codes < TI * TJ
    tile_position = jnp.where(active_flag, owner_col * TI + pair_codes // TJ, 0).astype(jnp.int32)
    column_position = (row_index * TJ + pair_codes % TJ).astype(jnp.int32)
    return (block_data[..., :RANK], block_data[..., RANK:], tile_position, column_position, active_flag.astype(jnp.float32))

def reference(slot_factors, slot_pairs, pivot_factors, a_factors, diag_factor, sketch):
    precise_mode = lax.Precision.HIGHEST
    pivot_data = pivot_factors.astype(jnp.float32)
    pivot_left_factor = pivot_data[..., :RANK]
    pivot_right_factor = pivot_data[..., RANK:]
    weights = jnp.einsum('jbr,bc->jrc', pivot_left_factor, sketch, precision=precise_mode)
    a_data = a_factors.astype(jnp.float32)
    a_left = a_data[..., :RANK]
    a_right = a_data[..., RANK:]
    a_sketch = jnp.einsum('ibr,bc->irc', a_right, sketch, precision=precise_mode)
    y_a = jnp.einsum('ibr,irc->ibc', a_left, a_sketch, precision=precise_mode)

    def first_pass(row_index, totals):
        slot_left_factor, slot_right_factor, tile_position, column_position, active_flag = slot_block(slot_factors, slot_pairs, row_index)
        coupling_matrix = jnp.einsum('jzk,jzu->jku', slot_right_factor, pivot_right_factor[column_position], precision=precise_mode)
        panel_kernel = jnp.einsum('src,scd->srd', coupling_matrix, weights[column_position], precision=precise_mode)
        update_contribution = jnp.einsum('gxn,gny->gxy', slot_left_factor, panel_kernel, precision=precise_mode) * active_flag[:, None, None]
        return totals.at[tile_position].add(update_contribution)
    zeros = jnp.zeros((ROWS_T, TILE, RANK), jnp.float32)
    y_sum = lax.fori_loop(0, N_ROW, first_pass, zeros)
    basis_column_count = orthonormal(y_a - y_sum)

    def second_pass(row_index, totals):
        slot_left_factor, slot_right_factor, tile_position, column_position, active_flag = slot_block(slot_factors, slot_pairs, row_index)
        coupling_matrix = jnp.einsum('jzk,jzu->jku', slot_right_factor, pivot_right_factor[column_position], precision=precise_mode)
        inner_product = jnp.einsum('jzk,jzu->jku', slot_left_factor, basis_column_count[tile_position], precision=precise_mode)
        reduced = jnp.einsum('src,srd->scd', coupling_matrix, inner_product, precision=precise_mode)
        lifted = jnp.einsum('sbc,scd->sbd', pivot_left_factor[column_position], reduced, precision=precise_mode)
        return totals.at[tile_position].add(lifted * active_flag[:, None, None])
    m_sum = lax.fori_loop(0, N_ROW, second_pass, zeros)
    m_a = jnp.einsum('ibr,irc->ibc', a_right, jnp.einsum('ibr,ibc->irc', a_left, basis_column_count, precision=precise_mode), precision=precise_mode)
    projected = m_a - m_sum
    stacked = jnp.transpose(projected, (1, 0, 2)).reshape(TILE, ROWS_T * RANK)
    solved = lax.linalg.triangular_solve(diag_factor, stacked, left_side=True, lower=True)
    coefficient = jnp.transpose(solved.reshape(TILE, ROWS_T, RANK), (1, 0, 2))
    root_tile = jnp.sqrt(jnp.float32(TILE))
    return (basis_column_count * root_tile, coefficient / root_tile)
```

```python
import math

import jax
import jax.numpy as jnp
from jax import lax
from jax.experimental import pallas as pl
from jax.experimental.pallas import tpu as pltpu
from jax.sharding import PartitionSpec as P

F32 = jnp.float32
BF16 = jnp.bfloat16
HIGHEST = lax.Precision.HIGHEST
PIECES = 65
SUB = 32
BLOCK = 256


def mm(a, b, ca=1, cb=0, precision=None):
    dims = (((ca,), (cb,)), ((), ()))
    return lax.dot_general(a, b, dims, precision=precision, preferred_element_type=F32)


def split3(x):
    hi = x.astype(BF16)
    rest = x - hi.astype(F32)
    mid = rest.astype(BF16)
    lo = (rest - mid.astype(F32)).astype(BF16)
    return hi, mid, lo


def mixed(a, parts, ca=1, cb=0):
    hi, mid, lo = parts
    return mm(a, lo, ca, cb) + mm(a, mid, ca, cb) + mm(a, hi, ca, cb)


def inverse_cholesky(gram):
    n = gram.shape[0]
    lane = lax.broadcasted_iota(jnp.int32, (8, n), 1)
    row = lax.broadcasted_iota(jnp.int32, (8, n), 0)
    tiles = [gram[8 * t : 8 * t + 8, :] for t in range(n // 8)]
    for k in range(n):
        t0, kk = divmod(k, 8)
        cols = {t: jnp.broadcast_to(tiles[t][:, k : k + 1], (8, n)) for t in range(t0, n // 8)}
        pivot = cols[t0][kk : kk + 1, :]
        here = tiles[t0][kk : kk + 1, :]
        cleared = jnp.where(lane[:1] == k, 1.0, here)
        scaled = cleared / pivot
        head = tiles[t0]
        eliminated = jnp.where(lane == k, 0.0, head) - cols[t0] * scaled
        final = jnp.where(lane <= k, cleared * lax.rsqrt(pivot), 0.0)
        tiles[t0] = jnp.where(row > kk, eliminated, jnp.where(row == kk, final, head))
        for t in range(t0 + 1, n // 8):
            tiles[t] = jnp.where(lane == k, 0.0, tiles[t]) - cols[t] * scaled
    return jnp.concatenate(tiles, axis=0)


def diag_inverse_kernel(d_ref, x_ref):
    n = d_ref.shape[0]
    rank = 128
    blocks = n // rank
    groups = rank // SUB
    lane = lax.broadcasted_iota(jnp.int32, (SUB, rank), 1)
    packed = []
    for b in range(blocks):
        acc = jnp.zeros((SUB, rank), F32)
        for g in range(groups):
            part = d_ref[rank * b + SUB * g : rank * b + SUB * (g + 1), rank * b : rank * (b + 1)]
            acc = jnp.where(lane // SUB == g, part, acc)
        packed.append(acc)
    lane8 = lax.broadcasted_iota(jnp.int32, (8, rank), 1)
    row8 = lax.broadcasted_iota(jnp.int32, (8, rank), 0)
    steps = SUB // 8
    low = [[packed[b][8 * t : 8 * t + 8] for t in range(steps)] for b in range(blocks)]
    inv = [
        [jnp.where(lane8 % SUB == row8 + 8 * t, 1.0, 0.0) for t in range(steps)] for b in range(blocks)
    ]
    for k in range(SUB):
        t0, kk = divmod(k, 8)
        index = (lane8 // SUB) * SUB + k
        for b in range(blocks):
            coef = {t: jnp.take_along_axis(low[b][t], index, axis=1) for t in range(t0, steps)}
            pivot_row = inv[b][t0][kk : kk + 1] / coef[t0][kk : kk + 1]
            head = inv[b][t0]
            head = jnp.where(row8 > kk, head - coef[t0] * pivot_row, head)
            inv[b][t0] = jnp.where(row8 == kk, pivot_row, head)
            for t in range(t0 + 1, steps):
                inv[b][t] = inv[b][t] - coef[t] * pivot_row
    row_full = lax.broadcasted_iota(jnp.int32, (rank, rank), 0)
    lane_full = lax.broadcasted_iota(jnp.int32, (rank, rank), 1)
    whole = []
    for b in range(blocks):
        small = jnp.concatenate(inv[b], axis=0)
        x = jnp.concatenate([jnp.where(lane // SUB == g, small, 0.0) for g in range(groups)], axis=0)
        d = d_ref[rank * b : rank * (b + 1), rank * b : rank * (b + 1)]
        size = SUB
        while size < rank:
            below = ((row_full // size) % 2 == 1) & (lane_full // size == row_full // size - 1)
            off = jnp.where(below, d, 0.0)
            x = x - mm(x, mm(off, x, precision=HIGHEST), precision=HIGHEST)
            size *= 2
        whole.append(x)
    for p in range(blocks // 2):
        first, second = whole[2 * p], whole[2 * p + 1]
        base = BLOCK * p
        off = d_ref[base + rank : base + BLOCK, base : base + rank]
        cross = mm(second, mm(off, first, precision=HIGHEST), precision=HIGHEST)
        x_ref[p, :rank, :rank] = first
        x_ref[p, :rank, rank:] = jnp.zeros((rank, rank), F32)
        x_ref[p, rank:, :rank] = -cross
        x_ref[p, rank:, rank:] = second


def first_kernel(code_ref, row_ref, slot_ref, pivot_ref, a_ref, sketch_ref, y_ref, c_ref):
    rank = sketch_ref.shape[1]
    earlier = pivot_ref.shape[0]
    slots = slot_ref.shape[0]
    sketch = split3(sketch_ref[...])
    weights = [mixed(pivot_ref[j, :, :rank], sketch, 0, 0) for j in range(earlier)]
    kernels = []
    for s in range(slots):
        code = code_ref[s]
        live = code < earlier
        j = jnp.where(live, code, 0)
        coupling = mm(slot_ref[s, :, rank:], pivot_ref[j, :, rank:], 0, 0)
        c_ref[s] = coupling
        weight = weights[0]
        for other in range(1, earlier):
            weight = jnp.where(j == other, weights[other], weight)
        kernels.append(jnp.where(live, mm(coupling, weight, precision=HIGHEST), 0.0))
    left = jnp.concatenate([slot_ref[s, :, :rank] for s in range(slots)], axis=1)
    y_ref[...] = -mixed(left, split3(jnp.concatenate(kernels, axis=0)))
    a_sketch = split3(mixed(a_ref[:, rank:], sketch, 0, 0))
    mine = pl.ds(pl.multiple_of(row_ref[0] * CHUNK, CHUNK), CHUNK)
    y_ref[mine, :] = y_ref[mine, :] + mixed(a_ref[mine, :rank], a_sketch)


def second_kernel(code_ref, row_ref, *refs):
    pieces, (slot_hbm, pivot_hbm, a_hbm, c_ref, basis_ref, m_ref, slot_ref, pivot_ref, a_ref, y_ref, sems) = refs[:PIECES], refs[PIECES:]
    tile, rank = basis_ref.shape
    earlier = pivot_ref.shape[0]
    slots = slot_ref.shape[0]
    pairs = [
        (piece, y_ref.at[pl.ds(start, end - start)])
        for piece, (start, end) in zip(pieces, block_rows(tile))
    ]
    pairs += [(slot_hbm, slot_ref), (pivot_hbm, pivot_ref), (a_hbm, a_ref)]
    loads = [pltpu.make_async_copy(src, dst, sems.at[i]) for i, (src, dst) in enumerate(pairs)]
    for load in loads:
        load.start()
    for load in loads[:PIECES]:
        load.wait()
    y = y_ref[...]
    gram = mm(y, y, 0, 0, HIGHEST)
    q = mm(y, inverse_cholesky(gram), 1, 1, HIGHEST)
    basis_ref[...] = q * math.sqrt(tile)
    parts = split3(q)
    for load in loads[PIECES:]:
        load.wait()
    left = jnp.concatenate([slot_ref[s, :, :rank] for s in range(slots)], axis=1)
    inner = mixed(left, parts, 0, 0)
    lifted = [jnp.zeros((rank, rank), F32) for _ in range(earlier)]
    for s in range(slots):
        code = code_ref[s]
        reduced = mm(c_ref[s], inner[rank * s : rank * (s + 1)], 0, 0, HIGHEST)
        for j in range(earlier):
            lifted[j] = lifted[j] + jnp.where(code == j, reduced, 0.0)
    pivot_left = jnp.concatenate([pivot_ref[j, :, :rank] for j in range(earlier)], axis=1)
    m_ref[...] = -mixed(pivot_left, split3(jnp.concatenate(lifted, axis=0)))
    a_inner = split3(mixed(a_ref[:, :rank], parts, 0, 0))
    mine = pl.ds(pl.multiple_of(row_ref[0] * CHUNK, CHUNK), CHUNK)
    m_ref[mine, :] = m_ref[mine, :] + mixed(a_ref[mine, rank:], a_inner)


def solve_kernel(d_ref, x_ref, *refs):
    pieces, n_ref = refs[:-1], refs[-1]
    tile = n_ref.shape[0]
    m = jnp.concatenate([piece[...] for piece in pieces], axis=0)
    solved = None
    for b in range(tile // BLOCK):
        rows = slice(BLOCK * b, BLOCK * (b + 1))
        right = m[rows]
        if b:
            right = right - mm(d_ref[rows, : BLOCK * b], solved, precision=HIGHEST)
        block = mm(x_ref[b], right, precision=HIGHEST)
        solved = block if solved is None else jnp.concatenate([solved, block], axis=0)
        n_ref[rows, :] = block * (1.0 / math.sqrt(tile))


CHUNK = 64


def call(kernel, out_shape, scalars, far, arrays, loaded=()):
    vmem = pl.BlockSpec(memory_space=pltpu.VMEM)
    scratch = [pltpu.VMEM(x.shape, x.dtype) for x in loaded]
    if far:
        scratch.append(pltpu.SemaphoreType.DMA((len(far),)))
    return pl.pallas_call(
        kernel,
        out_shape=out_shape,
        in_specs=[pl.BlockSpec(memory_space=pltpu.SMEM)] * len(scalars)
        + [pl.BlockSpec(memory_space=pl.ANY)] * len(far)
        + [vmem] * len(arrays),
        out_specs=jax.tree.map(lambda _: vmem, out_shape),
        scratch_shapes=scratch,
        compiler_params=pltpu.CompilerParams(vmem_limit_bytes=(56 if far else 40) * 1024 * 1024),
    )(*scalars, *far, *arrays)


def block_rows(tile):
    tiles = tile // 8
    bounds = [8 * (i * tiles // PIECES) for i in range(PIECES + 1)]
    return list(zip(bounds[:-1], bounds[1:]))


def summed(x):
    return lax.psum(tuple(x[start:end] for start, end in block_rows(x.shape[0])), "row")


def gather_pivot(pivot_factors, cols):
    earlier, depth, width = pivot_factors.shape
    chips = cols // 2
    same_core = [[2 * i + core for i in range(chips)] for core in range(2)]
    same_chip = [[2 * i, 2 * i + 1] for i in range(chips)]
    copies = jnp.broadcast_to(pivot_factors[None], (chips, earlier, depth, width))
    mine = lax.all_to_all(copies, "col", 0, 0, tiled=True, axis_index_groups=same_core)
    other = lax.ppermute(mine, "col", [(i, i ^ 1) for i in range(cols)])
    core = lax.axis_index("col") % 2
    both = jnp.stack([jnp.where(core == 0, mine, other), jnp.where(core == 0, other, mine)], axis=1)
    return jnp.transpose(both, (2, 0, 1, 3, 4)).reshape(earlier, cols * depth, width)


def make(rows, cols):
    def shards(slot_factors, slot_pairs, pivot_factors, a_factors, diag_factor, sketch):
        tile, rank = sketch.shape
        slots = slot_factors.shape[2]
        whole = jax.ShapeDtypeStruct((tile, rank), F32)
        codes = slot_pairs.reshape(slots)
        row = lax.axis_index("row").astype(jnp.int32).reshape(1)
        slot_data = slot_factors[0, 0]
        a_data = a_factors[0]
        inverse_shape = jax.ShapeDtypeStruct((tile // BLOCK, BLOCK, BLOCK), F32)
        inverse = call(diag_inverse_kernel, inverse_shape, (), (), (diag_factor,))
        pivot = gather_pivot(pivot_factors, cols)
        y_part, coupling = call(
            first_kernel,
            (whole, jax.ShapeDtypeStruct((slots, rank, rank), F32)),
            (codes, row),
            (),
            (slot_data, pivot, a_data, sketch),
        )
        basis, m_part = call(
            second_kernel,
            (whole, whole),
            (codes, row),
            (*summed(y_part), slot_data, pivot, a_data),
            (coupling,),
            (slot_data, pivot, a_data, whole),
        )
        coefficient = call(solve_kernel, whole, (), (), (diag_factor, inverse, *summed(m_part)))
        return basis[None], coefficient[None]

    return shards


def solution(mesh):
    in_specs = (
        P("row", "col", None, None, None),
        P("row", "col", None),
        P("row", "col", None),
        P("col", None, None),
        P(),
        P(),
    )
    out_specs = (P("col", None, None), P("col", None, None))
    body = make(mesh.shape["row"], mesh.shape["col"])
    return jax.shard_map(body, mesh=mesh, in_specs=in_specs, out_specs=out_specs, check_vma=False)
```

```python
import math

import jax
import jax.numpy as jnp
from jax import lax
from jax.experimental import pallas as pl
from jax.experimental.pallas import tpu as pltpu
from jax.sharding import PartitionSpec as P

F32 = jnp.float32
BF16 = jnp.bfloat16
HIGHEST = lax.Precision.HIGHEST
PIECES = 65
SUB = 32
BLOCK = 256


def mm(a, b, ca=1, cb=0, precision=None):
    dims = (((ca,), (cb,)), ((), ()))
    return lax.dot_general(a, b, dims, precision=precision, preferred_element_type=F32)


def split3(x):
    hi = x.astype(BF16)
    rest = x - hi.astype(F32)
    mid = rest.astype(BF16)
    lo = (rest - mid.astype(F32)).astype(BF16)
    return hi, mid, lo


def mixed(a, parts, ca=1, cb=0):
    hi, mid, lo = parts
    return mm(a, lo, ca, cb) + mm(a, mid, ca, cb) + mm(a, hi, ca, cb)


def mm3(a, b):
    (a_hi, a_lo, _), (b_hi, b_lo, _) = split3(a), split3(b)
    return mm(a_lo, b_hi) + mm(a_hi, b_lo) + mm(a_hi, b_hi)


def inverse_cholesky(gram):
    n = gram.shape[0]
    wide = (8, n)
    lane = lax.broadcasted_iota(jnp.int32, wide, 1)
    row = lax.broadcasted_iota(jnp.int32, wide, 0)
    tiles = [gram[8 * t : 8 * t + 8, :] for t in range(n // 8)]
    for p in range(n // 8):
        inside = lane // 8 == p
        head = tiles[p]
        columns = [jnp.broadcast_to(head[:, 8 * p + j : 8 * p + j + 1], wide) for j in range(8)]
        square = [[jnp.broadcast_to(columns[j][i : i + 1, :], wide) for j in range(i + 1)] for i in range(8)]
        rows = [
            jnp.where(inside, jnp.where(lane == 8 * p + i, 1.0, 0.0), jnp.broadcast_to(head[i : i + 1, :], wide))
            for i in range(8)
        ]
        ratios, inverses = {}, []
        for j in range(8):
            inverses.append(1.0 / square[j][j])
            below = [square[i][j] for i in range(8)[j + 1 :]]
            for i in range(j + 1, 8):
                ratios[i, j] = square[i][j] * inverses[j]
                for m in range(j + 1, i + 1):
                    square[i][m] = square[i][m] - ratios[i, j] * below[m - j - 1]
                rows[i] = rows[i] - ratios[i, j] * rows[j]
        solved = [None] * 8
        for i in reversed(range(8)):
            solved[i] = rows[i] * inverses[i]
            for j in range(i + 1, 8):
                solved[i] = solved[i] - ratios[j, i] * solved[j]
        final = rows[0] * lax.rsqrt(square[0][0])
        for i in range(1, 8):
            final = jnp.where(row == i, rows[i] * lax.rsqrt(square[i][i]), final)
        tiles[p] = jnp.where(lane <= row + 8 * p, final, 0.0)
        for t in range(p + 1, n // 8):
            old = tiles[t]
            terms = [jnp.broadcast_to(old[:, 8 * p + i : 8 * p + i + 1], wide) * solved[i] for i in range(8)]
            while len(terms) > 1:
                terms = [a + b for a, b in zip(terms[::2], terms[1::2])]
            tiles[t] = jnp.where(inside, 0.0, old) - terms[0]
    return jnp.concatenate(tiles, axis=0)


def diag_inverse_kernel(d_hbm, x_ref, d_ref, sems):
    n = d_hbm.shape[0]
    loads = []
    for p in range(n // BLOCK):
        part = pl.ds(BLOCK * p, BLOCK)
        loads.append(pltpu.make_async_copy(d_hbm.at[part, part], d_ref.at[part], sems.at[p]))
    for load in loads:
        load.start()
    for load in loads:
        load.wait()

    def block(start, size, column, width):
        base = start // BLOCK * BLOCK
        return d_ref[start : start + size, column - base : column - base + width]

    rank = 128
    blocks = n // rank
    groups = rank // SUB
    lane = lax.broadcasted_iota(jnp.int32, (SUB, rank), 1)
    packed = []
    for b in range(blocks):
        acc = jnp.zeros((SUB, rank), F32)
        for g in range(groups):
            part = block(rank * b + SUB * g, SUB, rank * b, rank)
            acc = jnp.where(lane // SUB == g, part, acc)
        packed.append(acc)
    lane8 = lax.broadcasted_iota(jnp.int32, (8, rank), 1)
    row8 = lax.broadcasted_iota(jnp.int32, (8, rank), 0)
    steps = SUB // 8
    low = [[packed[b][8 * t : 8 * t + 8] for t in range(steps)] for b in range(blocks)]
    inv = [
        [jnp.where(lane8 % SUB == row8 + 8 * t, 1.0, 0.0) for t in range(steps)] for b in range(blocks)
    ]
    for k in range(SUB):
        t0, kk = divmod(k, 8)
        index = (lane8 // SUB) * SUB + k
        for b in range(blocks):
            coef = {t: jnp.take_along_axis(low[b][t], index, axis=1) for t in range(t0, steps)}
            pivot_row = inv[b][t0][kk : kk + 1] / coef[t0][kk : kk + 1]
            head = inv[b][t0]
            head = jnp.where(row8 > kk, head - coef[t0] * pivot_row, head)
            inv[b][t0] = jnp.where(row8 == kk, pivot_row, head)
            for t in range(t0 + 1, steps):
                inv[b][t] = inv[b][t] - coef[t] * pivot_row
    row_full = lax.broadcasted_iota(jnp.int32, (rank, rank), 0)
    lane_full = lax.broadcasted_iota(jnp.int32, (rank, rank), 1)
    whole = []
    for b in range(blocks):
        small = jnp.concatenate(inv[b], axis=0)
        x = jnp.concatenate([jnp.where(lane // SUB == g, small, 0.0) for g in range(groups)], axis=0)
        d = block(rank * b, rank, rank * b, rank)
        size = SUB
        while size < rank:
            below = ((row_full // size) % 2 == 1) & (lane_full // size == row_full // size - 1)
            off = jnp.where(below, d, 0.0)
            x = x - mm3(x, mm3(off, x))
            size *= 2
        whole.append(x)
    for p in range(blocks // 2):
        first, second = whole[2 * p], whole[2 * p + 1]
        base = BLOCK * p
        off = block(base + rank, rank, base, rank)
        cross = mm3(second, mm3(off, first))
        x_ref[p, :rank, :rank] = first
        x_ref[p, :rank, rank:] = jnp.zeros((rank, rank), F32)
        x_ref[p, rank:, :rank] = -cross
        x_ref[p, rank:, rank:] = second


def first_kernel(code_ref, row_ref, slot_ref, pivot_ref, a_ref, sketch_ref, y_ref, c_ref):
    rank = sketch_ref.shape[1]
    earlier = pivot_ref.shape[0]
    slots = slot_ref.shape[0]
    sketch = split3(sketch_ref[...])
    weights = [mixed(pivot_ref[j, :, :rank], sketch, 0, 0) for j in range(earlier)]
    kernels = []
    for s in range(slots):
        code = code_ref[s]
        live = code < earlier
        j = jnp.where(live, code, 0)
        coupling = mm(slot_ref[s, :, rank:], pivot_ref[j, :, rank:], 0, 0)
        c_ref[s] = coupling
        weight = weights[0]
        for other in range(1, earlier):
            weight = jnp.where(j == other, weights[other], weight)
        kernels.append(jnp.where(live, mm(coupling, weight, precision=HIGHEST), 0.0))
    left = jnp.concatenate([slot_ref[s, :, :rank] for s in range(slots)], axis=1)
    y_ref[...] = -mixed(left, split3(jnp.concatenate(kernels, axis=0)))
    a_sketch = split3(mixed(a_ref[:, rank:], sketch, 0, 0))
    mine = pl.ds(pl.multiple_of(row_ref[0] * CHUNK, CHUNK), CHUNK)
    y_ref[mine, :] = y_ref[mine, :] + mixed(a_ref[mine, :rank], a_sketch)


def second_kernel(code_ref, row_ref, *refs):
    pieces, outs = refs[:PIECES], refs[PIECES + 5 : 2 * PIECES + 5]
    slot_hbm, pivot_hbm, a_hbm, c_hbm, basis_ref = refs[PIECES : PIECES + 5]
    slot_ref, pivot_ref, a_ref, c_ref, y_ref, sems = refs[2 * PIECES + 5 :]
    tile, rank = basis_ref.shape
    earlier = pivot_ref.shape[0]
    slots = slot_ref.shape[0]
    pairs = [
        (piece, y_ref.at[pl.ds(start, end - start)])
        for piece, (start, end) in zip(pieces, block_rows(tile))
    ]
    pairs += [(slot_hbm, slot_ref), (pivot_hbm, pivot_ref), (a_hbm, a_ref), (c_hbm, c_ref)]
    loads = [pltpu.make_async_copy(src, dst, sems.at[i]) for i, (src, dst) in enumerate(pairs)]
    for load in loads:
        load.start()
    for load in loads[:PIECES]:
        load.wait()
    y = y_ref[...]
    gram = mm(y, y, 0, 0, HIGHEST)
    q = mm(y, inverse_cholesky(gram), 1, 1, HIGHEST)
    basis_ref[...] = q * math.sqrt(tile)
    parts = split3(q)
    for load in loads[PIECES:]:
        load.wait()
    left = jnp.concatenate([slot_ref[s, :, :rank] for s in range(slots)], axis=1)
    inner = mixed(left, parts, 0, 0)
    lifted = [jnp.zeros((rank, rank), F32) for _ in range(earlier)]
    for s in range(slots):
        code = code_ref[s]
        reduced = mm(c_ref[s], inner[rank * s : rank * (s + 1)], 0, 0, HIGHEST)
        for j in range(earlier):
            lifted[j] = lifted[j] + jnp.where(code == j, reduced, 0.0)
    pivot_left = jnp.concatenate([pivot_ref[j, :, :rank] for j in range(earlier)], axis=1)
    y_ref[...] = -mixed(pivot_left, split3(jnp.concatenate(lifted, axis=0)))
    a_inner = split3(mixed(a_ref[:, :rank], parts, 0, 0))
    mine = pl.ds(pl.multiple_of(row_ref[0] * CHUNK, CHUNK), CHUNK)
    y_ref[mine, :] = y_ref[mine, :] + mixed(a_ref[mine, rank:], a_inner)
    stores = [
        pltpu.make_async_copy(y_ref.at[pl.ds(start, end - start)], out, sems.at[i])
        for i, (out, (start, end)) in enumerate(zip(outs, block_rows(tile)))
    ]
    for store in stores:
        store.start()
    for store in stores:
        store.wait()


def solve_kernel(d_hbm, x_hbm, *refs):
    pieces, (n_ref, d_ref, x_ref, m_ref, sems) = refs[:PIECES], refs[PIECES:]
    tile = n_ref.shape[0]
    count = tile // BLOCK
    takes = [
        pltpu.make_async_copy(piece, m_ref.at[pl.ds(start, end - start)], sems.at[i + count])
        for i, (piece, (start, end)) in enumerate(zip(pieces, block_rows(tile)))
    ]
    takes.append(pltpu.make_async_copy(x_hbm, x_ref, sems.at[0]))
    for take in takes:
        take.start()
    loads = []
    for b in range(1, count):
        part = pl.ds(BLOCK * b, BLOCK), pl.ds(0, BLOCK * b)
        loads.append(pltpu.make_async_copy(d_hbm.at[part], d_ref.at[part], sems.at[b]))
    for load in loads:
        load.start()
    for take in takes:
        take.wait()
    m = m_ref[...]
    solved = []
    for b in range(count):
        rows = slice(BLOCK * b, BLOCK * (b + 1))
        right = m[rows]
        if b:
            loads[b - 1].wait()
            right = right - mm3(d_ref[rows, : BLOCK * b], jnp.concatenate(solved, axis=0))
        solved.append(mm3(x_ref[b], right))
        n_ref[rows, :] = solved[b] * (1.0 / math.sqrt(tile))


CHUNK = 64


def call(kernel, out_shape, scalars, far, arrays, loaded=(), grant=56, blocks=()):
    vmem = pl.BlockSpec(memory_space=pltpu.VMEM)
    scratch = [pltpu.VMEM(x.shape, x.dtype) for x in loaded]
    if far:
        scratch.append(pltpu.SemaphoreType.DMA((len(far) + 8,)))
    return pl.pallas_call(
        kernel,
        out_shape=[*out_shape, *blocks],
        in_specs=[pl.BlockSpec(memory_space=pltpu.SMEM)] * len(scalars)
        + [pl.BlockSpec(memory_space=pl.ANY)] * len(far)
        + [vmem] * len(arrays),
        out_specs=[vmem] * len(out_shape) + [pl.BlockSpec(memory_space=pl.ANY)] * len(blocks),
        scratch_shapes=scratch,
        compiler_params=pltpu.CompilerParams(vmem_limit_bytes=grant * 1024 * 1024),
    )(*scalars, *far, *arrays)


def block_rows(tile):
    tiles = tile // 8
    bounds = [8 * (i * tiles // PIECES) for i in range(PIECES + 1)]
    return list(zip(bounds[:-1], bounds[1:]))


def summed(blocks):
    return lax.psum(tuple(blocks), "row")


def gather_pivot(pivot_factors, cols):
    earlier, depth, width = pivot_factors.shape
    chips = cols // 2
    same_core = [[2 * i + core for i in range(chips)] for core in range(2)]
    same_chip = [[2 * i, 2 * i + 1] for i in range(chips)]
    copies = jnp.broadcast_to(pivot_factors[None], (chips, earlier, depth, width))
    mine = lax.all_to_all(copies, "col", 0, 0, tiled=True, axis_index_groups=same_core)
    other = lax.ppermute(mine, "col", [(i, i ^ 1) for i in range(cols)])
    core = lax.axis_index("col") % 2
    both = jnp.stack([jnp.where(core == 0, mine, other), jnp.where(core == 0, other, mine)], axis=1)
    return jnp.transpose(both, (2, 0, 1, 3, 4)).reshape(earlier, cols * depth, width)


def make(rows, cols):
    def shards(slot_factors, slot_pairs, pivot_factors, a_factors, diag_factor, sketch):
        tile, rank = sketch.shape
        slots = slot_factors.shape[2]
        whole = jax.ShapeDtypeStruct((tile, rank), F32)
        codes = slot_pairs.reshape(slots)
        row = lax.axis_index("row").astype(jnp.int32).reshape(1)
        slot_data = slot_factors[0, 0]
        a_data = a_factors[0]
        inverse_shape = jax.ShapeDtypeStruct((tile // BLOCK, BLOCK, BLOCK), F32)
        diagonal = jax.ShapeDtypeStruct((tile, BLOCK), F32)
        blocks = [jax.ShapeDtypeStruct((end - start, rank), F32) for start, end in block_rows(tile)]
        (inverse,) = call(diag_inverse_kernel, [inverse_shape], (), (diag_factor,), (), (diagonal,))
        pivot = gather_pivot(pivot_factors, cols)
        y_part, coupling = call(
            first_kernel,
            [whole, jax.ShapeDtypeStruct((slots, rank, rank), F32)],
            (codes, row),
            (),
            (slot_data, pivot, a_data, sketch),
            grant=40,
        )
        basis, *m_part = call(
            second_kernel,
            [whole],
            (codes, row),
            (
                *summed(y_part[start:end] for start, end in block_rows(tile)),
                slot_data,
                pivot,
                a_data,
                coupling,
            ),
            (),
            (slot_data, pivot, a_data, coupling, whole),
            blocks=blocks,
        )
        (coefficient,) = call(
            solve_kernel,
            [whole],
            (),
            (diag_factor, inverse, *summed(m_part)),
            (),
            (diag_factor, inverse_shape, whole),
        )
        return basis[None], coefficient[None]

    return shards


def solution(mesh):
    in_specs = (
        P("row", "col", None, None, None),
        P("row", "col", None),
        P("row", "col", None),
        P("col", None, None),
        P(),
        P(),
    )
    out_specs = (P("col", None, None), P("col", None, None))
    body = make(mesh.shape["row"], mesh.shape["col"])
    return jax.shard_map(body, mesh=mesh, in_specs=in_specs, out_specs=out_specs, check_vma=False)
```
